32 devices in a mesh: row: 8 (over y, x, core), col: 4 (over z).
Axes of the slice: x: 2, y: 2, z: 4, core: 2. Of those that a mesh axis runs over, the one named last changes fastest.
Arguments:
- shear_stress: float32 [512, 16384], P(None, ('row', 'col')), may hold values from -3.5 to 3.5
- state_var: float32 [512, 16384], P(None, ('row', 'col')), may hold values from -0.4 to 0.4
- a_param: float32 [16384], P(('row', 'col')), may hold values from 0.7 to 1.4
- rate_param: float32 [16384], P(('row', 'col')), may hold values from 0.1 to 0.5
- loading: float32 [16384], P(('row', 'col')), may hold values from 0.1 to 1
- dense_tiles: bfloat16 [16384, 16384], P('row', 'col'), may hold values from -0.046875 to 0.046875
- left_factor: bfloat16 [512, 16384], P('col', 'row'), may hold values from -0.75 to 0.75
- right_factor: bfloat16 [512, 16384], P('row', 'col'), may hold values from -0.046875 to 0.046875
- admissible: int32 [8, 8], replicated, may hold values from 0 to 1, as said below
- tile_ranks: int32 [8, 8], replicated, may hold values from 16 to 64
Outputs:
- shear_next: float32 [512, 16384], P(None, ('row', 'col'))
- state_next: float32 [512, 16384], P(None, ('row', 'col'))
The draws below stay inside these ranges and needn't reach their ends.
Inputs may be any that keep to these rules, and one draw needn't show every extreme that they name: `admissible`: tiles on the diagonal and next to it are always dense; elsewhere a tile is dense or low-rank at random.
All inputs are finite; a program needn't handle non-finite values.
Results may differ from the reference program's by a relative error of at most 0.0024.
Values may be sent and summed in bfloat16 or wider, within the bound.
A program may use at most 128 MiB of HBM per device.

```python
import math
import jax
import jax.numpy as jnp
from jax import lax

TILE = 2048
RANK = 64
SCEN = 512
NB = 8
N = 16384


def draw_admissible(key, part):
    index_line = jnp.arange(NB, dtype=jnp.int32)
    nearby = jnp.abs(index_line[:, None] - index_line[None, :]) <= 1
    coins = jax.random.randint(key, (NB, NB), 0, 4) == 0
    return jnp.where(nearby | coins, 1, 0).astype(jnp.int32)


def touch_ends(array, key, smallest, largest):
    shape = array.shape
    index_at = [jax.random.randint(jax.random.fold_in(key, axis), (), 0, shape[axis]) for axis in range(len(shape))]
    array = array.at[tuple(index_at)].set(smallest)
    longest = shape.index(max(shape))
    index_at[longest] = (index_at[longest] + 1) % shape[longest]
    return array.at[tuple(index_at)].set(largest)


def steps_of(stream_key, dims, split, low, high):
    gain, own = 1.0, jax.random.fold_in(stream_key, 6)
    for position, blocks in split:
        heights = jnp.exp(jax.random.uniform(jax.random.fold_in(own, position), (blocks,), jnp.float32, low / len(split), high / len(split)))
        gain = gain * jnp.repeat(heights, dims[position] // blocks).reshape([-1 if axis == position else 1 for axis in range(len(dims))])
    return gain


def normal_values(key, extent, scale, bound, pieces=(), kind=jnp.bfloat16):
    array = scale * jax.random.normal(key, extent, jnp.float32)
    if pieces:
        array = array * steps_of(key, extent, pieces, -0.22, 0.18)
    return jnp.clip(array, -bound, bound).astype(kind)


def setup_inputs(seed: int = 0) -> dict:
    key_of = jax.random.split(jax.random.key(seed), 11)
    shear_stress = normal_values(key_of[0], (SCEN, N), 0.4, 3.5, ((1, 32),), jnp.float32)
    state_var = jnp.clip(jax.random.uniform(key_of[1], (SCEN, N), jnp.float32, -0.4, 0.4) * steps_of(key_of[1], (SCEN, N), ((1, 32),), -0.4, 0.0), -0.4, 0.4)
    a_param = jnp.clip(jnp.exp(math.log(1.4) - 0.6931472 * jax.random.uniform(key_of[2], (N,), jnp.float32) ** steps_of(key_of[2], (N,), ((0, 32),), -0.2, 0.2)), 0.7, 1.4)
    rate_param = jnp.clip(jnp.exp(math.log(0.5) - 1.609438 * jax.random.uniform(key_of[3], (N,), jnp.float32) ** steps_of(key_of[3], (N,), ((0, 32),), -0.2, 0.2)), 0.1, 0.5)
    loading = jnp.clip(jnp.exp(math.log(1.0) - 2.3025851 * jax.random.uniform(key_of[4], (N,), jnp.float32) ** steps_of(key_of[4], (N,), ((0, 32),), -0.2, 0.2)), 0.1, 1.0)
    dense_tiles = normal_values(key_of[5], (N, N), N ** -0.5, 0.046875, ((0, 8), (1, 4)))
    left_factor = normal_values(key_of[6], (NB * RANK, N), RANK ** -0.5, 0.75, ((0, 4), (1, 8)))
    right_factor = normal_values(key_of[7], (NB * RANK, N), N ** -0.5, 0.046875, ((0, 8), (1, 4)))
    admissible = draw_admissible(jax.random.fold_in(key_of[10], 71), 0)
    tile_ranks = touch_ends(jax.random.randint(key_of[9], (NB, NB), RANK // 4, RANK + 1), jax.random.fold_in(key_of[9], 1), RANK // 4, RANK).astype(jnp.int32)
    return dict(shear_stress=shear_stress, state_var=state_var, a_param=a_param, rate_param=rate_param, loading=loading, dense_tiles=dense_tiles, left_factor=left_factor, right_factor=right_factor, admissible=admissible, tile_ranks=tile_ranks)


def slip_velocity(shear_now, state_now, a_param):
    return jnp.sinh(shear_now / a_param[None, :]) * jnp.exp(-state_now)


def tile_product(vec_tile, dense_tile, left_tile, right_tile, is_dense, rank_here):
    def dense_branch(operands):
        return lax.dot_general(operands[0], operands[1], (((1,), (1,)), ((), ())), preferred_element_type=jnp.float32)

    def factor_branch(operands):
        projection = lax.dot_general(operands[0], operands[3], (((1,), (1,)), ((), ())), preferred_element_type=jnp.float32)
        keep_mask = jnp.arange(projection.shape[1], dtype=jnp.int32)[None, :] < rank_here
        projection = jnp.where(keep_mask, projection, jnp.zeros_like(projection)).astype(jnp.bfloat16)
        return jnp.dot(projection, operands[2], preferred_element_type=jnp.float32)

    return lax.cond(is_dense == 1, dense_branch, factor_branch, (vec_tile, dense_tile, left_tile, right_tile))


def interaction(rounded, dense_tiles, left_factor, right_factor, admissible, tile_ranks):
    def target_row(row_tile):
        def source_col(accum_sum, col_tile):
            vec_tile = lax.dynamic_slice_in_dim(rounded, col_tile * TILE, TILE, 1)
            dense_tile = lax.dynamic_slice(dense_tiles, (row_tile * TILE, col_tile * TILE), (TILE, TILE))
            left_tile = lax.dynamic_slice(left_factor, (col_tile * RANK, row_tile * TILE), (RANK, TILE))
            right_tile = lax.dynamic_slice(right_factor, (row_tile * RANK, col_tile * TILE), (RANK, TILE))
            term = tile_product(vec_tile, dense_tile, left_tile, right_tile, admissible[row_tile, col_tile], tile_ranks[row_tile, col_tile])
            return accum_sum + term, None

        accum_sum, unused_out = lax.scan(source_col, jnp.zeros((SCEN, TILE), jnp.float32), jnp.arange(NB, dtype=jnp.int32))
        return accum_sum

    blocks = lax.map(target_row, jnp.arange(NB, dtype=jnp.int32))
    return jnp.transpose(blocks, (1, 0, 2)).reshape(SCEN, N)


def reference(shear_stress, state_var, a_param, rate_param, loading, dense_tiles, left_factor, right_factor, admissible, tile_ranks):
    def rates(shear_now, state_now):
        velocity = slip_velocity(shear_now, state_now, a_param)
        rounded = velocity.astype(jnp.bfloat16)
        pushed = interaction(rounded, dense_tiles, left_factor, right_factor, admissible, tile_ranks)
        k_shear = loading[None, :] - pushed
        k_state = rate_param[None, :] * (jnp.exp(-state_now) - jnp.abs(velocity))
        return k_shear, k_state

    k_shear1, k_state1 = rates(shear_stress, state_var)
    shear_mid = shear_stress + 0.5 * k_shear1
    state_mid = state_var + 0.5 * k_state1
    k_shear2, k_state2 = rates(shear_mid, state_mid)
    shear_next = shear_stress + 0.25 * (k_shear1 + k_shear2)
    state_next = state_var + 0.25 * (k_state1 + k_state2)
    return (shear_next, state_next)
```

```python
import functools
import math

import jax
import jax.numpy as jnp
from jax import lax
from jax.experimental import pallas as pl
from jax.experimental.pallas import tpu as pltpu
from jax.sharding import PartitionSpec as P

TILE = 2048
RANK = 64
GROUP = 16
LAG = 4
LN2 = math.log(2.0)
MESH = pl.DeviceIdType.MESH
F32 = jnp.float32
BF16 = jnp.bfloat16


def kernel(
    rows,
    cols,
    shear_hbm,
    state_hbm,
    a_ref,
    rate_ref,
    load_ref,
    dense_ref,
    left_ref,
    right_ref,
    adm_ref,
    rank_ref,
    shear_out,
    state_out,
    weights,
    gathered,
    vsend,
    staged,
    partial,
    psend,
    precv,
    own,
    shear,
    state,
    k_shear,
    k_state,
    dense_sem,
    in_sem,
    out_sem,
    st_send,
    st_recv,
    p1_send,
    p1_recv,
    p2_send,
    p2_recv,
    sib_send,
    sib_recv,
    rs_send,
    rs_recv,
):
    scenarios, piece = shear.shape
    chunk = rows * GROUP
    chunks = scenarios // chunk
    units = 2 * chunks
    half = rows // 2
    per = rows // cols
    slots = partial.shape[0]
    r = lax.axis_index("row")
    c = lax.axis_index("col")
    mine = c * per
    sib = r + 1 - 2 * (r % 2)
    targets, sources = weights.shape
    across = sources // TILE
    build_rows = 256
    builds = targets // build_rows
    build_cols = 512
    low = c < cols // 2
    middle = (c > 0) & (c < cols - 1)

    def scen(q):
        return pl.ds(pl.multiple_of(q * chunk, chunk), chunk)

    def shear_in(q):
        return pltpu.make_async_copy(
            shear_hbm.at[scen(q), :], shear.at[scen(q), :], in_sem.at[0, q]
        )

    def state_in(q):
        return pltpu.make_async_copy(
            state_hbm.at[scen(q), :], state.at[scen(q), :], in_sem.at[1, q]
        )

    def shear_store(q):
        return pltpu.make_async_copy(
            shear.at[scen(q), :], shear_out.at[scen(q), :], out_sem.at[0, q]
        )

    def state_store(q):
        return pltpu.make_async_copy(
            state.at[scen(q), :], state_out.at[scen(q), :], out_sem.at[1, q]
        )

    def dense_in(b):
        span = pl.ds(pl.multiple_of(b * build_rows, build_rows), build_rows)
        return pltpu.make_async_copy(
            dense_ref.at[span, :], weights.at[span, :], dense_sem.at[b]
        )

    def group_of(u, g):
        return gathered.at[u, pl.ds(pl.multiple_of(g * GROUP, GROUP), GROUP), :]

    def part_of(u, g):
        return vsend.at[u, pl.ds(pl.multiple_of(g * GROUP, GROUP), GROUP), :]

    def st_copy(u, j):
        return pltpu.make_async_remote_copy(
            src_ref=part_of(u, j),
            dst_ref=staged.at[u, r],
            send_sem=st_send.at[u],
            recv_sem=st_recv.at[u],
            device_id=(j, c),
            device_id_type=MESH,
        )

    def place(u, source):
        slot = (source % per) * cols + c
        return gathered.at[
            u,
            pl.ds(pl.multiple_of(r * GROUP, GROUP), GROUP),
            pl.ds(pl.multiple_of(slot * piece, piece), piece),
        ]

    def p1_copy(u, source):
        return pltpu.make_async_remote_copy(
            src_ref=staged.at[u, source],
            dst_ref=place(u, source),
            send_sem=p1_send.at[u],
            recv_sem=p1_recv.at[u],
            device_id=(r, source // per),
            device_id_type=MESH,
        )

    def plane_copy(u, g, row_to):
        return pltpu.make_async_remote_copy(
            src_ref=group_of(u, g),
            dst_ref=group_of(u, g),
            send_sem=p2_send.at[u],
            recv_sem=p2_recv.at[u, g],
            device_id=(row_to, c),
            device_id_type=MESH,
        )

    def sib_copy(u, g):
        return pltpu.make_async_remote_copy(
            src_ref=group_of(u, g),
            dst_ref=group_of(u, g),
            send_sem=sib_send.at[u],
            recv_sem=sib_recv.at[u],
            device_id=(sib, c),
            device_id_type=MESH,
        )

    def rs_copy(u, d, up):
        to = jnp.where(up, c + 1, c - 1)
        slot = jnp.where(up | (d < to), d, cols)
        return pltpu.make_async_remote_copy(
            src_ref=psend.at[u, d],
            dst_ref=precv.at[u, slot],
            send_sem=rs_send.at[u],
            recv_sem=rs_recv.at[u, slot],
            device_id=(r, to),
            device_id_type=MESH,
        )

    def rs_arrival(u, slot):
        return pltpu.make_async_copy(
            precv.at[u, slot], precv.at[u, slot], rs_recv.at[u, slot]
        )

    inv_a = 1.0 / a_ref[...]

    def velocity(shear_now, state_now):
        x = shear_now * inv_a
        fade = jnp.exp(-state_now)
        v = (jnp.exp(x - LN2) - jnp.exp(-x - LN2)) * fade
        return v, rate_ref[...] * (fade - jnp.abs(v))

    def send_slip(u):
        def one(i, _):
            st_copy(u, (r + 1 + i) % rows).start()
            return 0

        lax.fori_loop(0, rows - 1, one, 0)
        pltpu.make_async_copy(part_of(u, r), staged.at[u, r], st_recv.at[u]).start()

    def relay(u):
        pltpu.make_async_copy(staged.at[u], staged.at[u], st_recv.at[u]).wait()

        def one(i, _):
            p1_copy(u, (mine + per + i) % rows).start()
            return 0

        lax.fori_loop(0, rows - per, one, 0)

        def stay(i, _):
            pltpu.make_async_copy(
                staged.at[u, mine + i], place(u, mine + i), p1_recv.at[u]
            ).start()
            return 0

        lax.fori_loop(0, per, stay, 0)

    def first_slip(q, _):
        shear_in(q).wait()
        state_in(q).wait()
        v, ks = velocity(shear[scen(q), :], state[scen(q), :])
        vsend[q] = v.astype(BF16)
        k_state[scen(q), :] = ks
        return 0

    def spread(u):
        pltpu.make_async_copy(group_of(u, r), group_of(u, r), p1_recv.at[u]).wait()

        def one(i, _):
            plane_copy(u, r, (r + 2 * (i + 1)) % rows).start()
            return 0

        lax.fori_loop(0, half - 1, one, 0)
        sib_copy(u, r).start()

    def forward(u):
        def one(i, _):
            g = (r + 2 * (i + 1)) % rows
            plane_copy(u, g, sib).wait_recv()
            sib_copy(u, g).start()
            return 0

        lax.fori_loop(0, half - 1, one, 0)

    def gather_end(u):
        span = pl.ds(0, half * GROUP)
        pltpu.make_async_copy(
            gathered.at[u, span, :], gathered.at[u, span, :], sib_recv.at[u]
        ).wait()

    def multiply(u, i):
        d = jnp.where(low, c + cols - 1 - i, c + 1 + i) % cols
        part = lax.dot_general(
            gathered[u],
            weights[pl.ds(pl.multiple_of(d * piece, piece), piece), :],
            (((1,), (1,)), ((), ())),
            preferred_element_type=F32,
        )

        @pl.when(d == c)
        def _():
            own[u % slots] = part

        @pl.when((d != c) & middle)
        def _():
            partial[u % slots, d] = part

        @pl.when((d != c) & jnp.logical_not(middle))
        def _():
            psend[u, d] = part.astype(BF16)
            rs_copy(u, d, c == 0).start()

    def hop(u, up):
        def one(i, _):
            d = jnp.where(up, cols - 1 - i, i)
            rs_arrival(u, d).wait()
            psend[u, d] = (partial[u % slots, d] + precv[u, d].astype(F32)).astype(BF16)
            rs_copy(u, d, up).start()
            return 0

        @pl.when(middle)
        def _():
            lax.fori_loop(0, jnp.where(up, cols - 1 - c, c), one, 0)

    def finish(u):
        @pl.when(c > 0)
        def _():
            rs_arrival(u, c).wait()
            own[u % slots] = own[u % slots] + precv[u, c].astype(F32)

        @pl.when(c < cols - 1)
        def _():
            rs_arrival(u, cols).wait()
            own[u % slots] = own[u % slots] + precv[u, cols].astype(F32)

        @pl.when(u < chunks)
        def _():
            here = scen(u)
            ks = load_ref[...] - own[u % slots]
            k_shear[here, :] = ks
            k1 = k_state[here, :]
            old = state[here, :]
            v, k2 = velocity(shear[here, :] + 0.5 * ks, old + 0.5 * k1)
            vsend[u + chunks] = v.astype(BF16)
            send_slip(u + chunks)
            state[here, :] = old + 0.25 * (k1 + k2)
            state_store(u).start()

        @pl.when(u >= chunks)
        def _():
            here = scen(u - chunks)
            ks = load_ref[...] - own[u % slots]
            shear[here, :] = shear[here, :] + 0.25 * (k_shear[here, :] + ks)
            shear_store(u - chunks).start()

    def build_order(i):
        if builds % cols:
            return i
        each = builds // cols
        d = jnp.where(low, c + cols - 1 - i // each, c + 1 + i // each) % cols
        return d * each + i % each

    def build(i, _):
        b = build_order(i)
        dense_in(b).wait()
        here = pl.ds(pl.multiple_of(b * build_rows, build_rows), build_rows)
        down = targets // TILE
        td = (b * build_rows) // TILE
        for k in range(across):
            dense = adm_ref[r * down + td, c * across + k]
            rank = rank_ref[r * down + td, c * across + k]
            kept = jnp.where(dense == 1, 0, rank)
            left = left_ref[k * RANK : (k + 1) * RANK, here]
            keep = lax.broadcasted_iota(jnp.int32, (RANK, build_rows), 0) < kept
            left = jnp.where(keep, left.astype(F32), 0.0)
            left = jnp.transpose(left).astype(BF16)
            scale = jnp.where(dense == 1, 1.0, 0.0).astype(F32)
            scale = jnp.full((build_rows, build_cols), scale, F32).astype(BF16)
            for s in range(TILE // build_cols):
                span = slice(k * TILE + s * build_cols, k * TILE + (s + 1) * build_cols)
                right = right_ref[pl.ds(pl.multiple_of(td * RANK, RANK), RANK), span]
                term = jnp.dot(left, right, preferred_element_type=F32).astype(BF16)
                weights[here, span] = weights[here, span] * scale + term
        return 0

    def drain(u):
        def sent(ref, sem):
            pltpu.make_async_copy(ref, ref, sem).wait()

        sent(vsend.at[u, pl.ds(0, (rows - 1) * GROUP), :], st_send.at[u])
        sent(staged.at[u, pl.ds(0, rows - per)], p1_send.at[u])
        sent(gathered.at[u, pl.ds(0, (half - 1) * GROUP), :], p2_send.at[u])
        sent(gathered.at[u, pl.ds(0, half * GROUP), :], sib_send.at[u])
        sent(psend.at[u, pl.ds(0, cols - 1)], rs_send.at[u])

    barrier = pltpu.get_barrier_semaphore()

    def greet_row(i, _):
        pl.semaphore_signal(
            barrier, inc=1, device_id=((r + 1 + i) % rows, c), device_id_type=MESH
        )
        return 0

    def greet_col(i, _):
        pl.semaphore_signal(
            barrier, inc=1, device_id=(r, (c + 1 + i) % cols), device_id_type=MESH
        )
        return 0

    lax.fori_loop(0, rows - 1, greet_row, 0)
    lax.fori_loop(0, cols - 1, greet_col, 0)

    def fetch(q, _):
        shear_in(q).start()
        state_in(q).start()
        return 0

    lax.fori_loop(0, chunks, fetch, 0)

    def fetch_dense(i, _):
        dense_in(build_order(i)).start()
        return 0

    lax.fori_loop(0, builds, fetch_dense, 0)
    lax.fori_loop(0, chunks, first_slip, 0)
    cuts = [builds * k // 8 for k in (0, 2, 4, 6, 8)]
    lax.fori_loop(cuts[0], cuts[1], build, 0)
    pl.semaphore_wait(barrier, rows + cols - 2)

    def first_send(q, _):
        send_slip(q)
        return 0

    lax.fori_loop(0, chunks, first_send, 0)
    lax.fori_loop(cuts[1], cuts[2], build, 0)

    def first_relay(q, _):
        relay(q)
        return 0

    lax.fori_loop(0, chunks, first_relay, 0)
    lax.fori_loop(cuts[2], cuts[3], build, 0)
    spread(0)
    spread(1)
    lax.fori_loop(cuts[3], cuts[4], build, 0)
    forward(0)

    gap = max(0, LAG - chunks)

    def at_slot(sigma, body, also=True):
        valid = ((sigma >= 0) & (sigma < chunks)) | (
            (sigma >= chunks + gap) & (sigma < units + gap)
        )

        @pl.when(valid & also)
        def _():
            body(jnp.where(sigma < chunks, sigma, sigma - gap))

    def step(t, _):
        at_slot(t - 1, lambda u: hop(u, low))
        early = t + 2 < chunks
        at_slot(jnp.where(early, t + 2, t + 1), spread, early | (t + 1 >= chunks))
        at_slot(t - 2, finish)
        at_slot(t, gather_end)

        def one(i, _):
            at_slot(t, lambda u: multiply(u, i))
            at_slot(t + 2, relay, (i == 0) & (t + 2 >= chunks))
            at_slot(t - 1, lambda u: hop(u, jnp.logical_not(low)), i == 1)
            return 0

        lax.fori_loop(0, cols, one, 0)
        at_slot(t + 1, forward)
        at_slot(t - 4, drain)
        return 0

    lax.fori_loop(0, units + gap + 2, step, 0)

    def last(u, _):
        drain(u)
        return 0

    lax.fori_loop(units - 2, units, last, 0)

    def stored(q, _):
        shear_store(q).wait()
        state_store(q).wait()
        return 0

    lax.fori_loop(0, chunks, stored, 0)


def solution(mesh):
    rows, cols = mesh.shape["row"], mesh.shape["col"]

    def on_device(
        shear, state, a_param, rate, loading, dense, left, right, admissible, ranks
    ):
        scenarios, piece = shear.shape
        chunk = rows * GROUP
        chunks = scenarios // chunk
        units = 2 * chunks
        slots = min(units, 4)
        vmem = pl.BlockSpec(memory_space=pltpu.VMEM)
        smem = pl.BlockSpec(memory_space=pltpu.SMEM)
        hbm = pl.BlockSpec(memory_space=pl.ANY)
        dma = pltpu.SemaphoreType.DMA
        return pl.pallas_call(
            functools.partial(kernel, rows, cols),
            out_shape=(
                jax.ShapeDtypeStruct(shear.shape, F32),
                jax.ShapeDtypeStruct(shear.shape, F32),
            ),
            in_specs=[hbm] * 2 + [vmem] * 3 + [hbm, vmem, vmem, smem, smem],
            out_specs=(hbm, hbm),
            scratch_shapes=[
                pltpu.VMEM(dense.shape, BF16),
                pltpu.VMEM((units, chunk, dense.shape[1]), BF16),
                pltpu.VMEM((units, chunk, piece), BF16),
                pltpu.VMEM((units, rows, GROUP, piece), BF16),
                pltpu.VMEM((slots, cols, chunk, piece), F32),
                pltpu.VMEM((units, cols, chunk, piece), BF16),
                pltpu.VMEM((units, cols + 1, chunk, piece), BF16),
                pltpu.VMEM((slots, chunk, piece), F32),
                pltpu.VMEM(shear.shape, F32),
                pltpu.VMEM(shear.shape, F32),
                pltpu.VMEM(shear.shape, F32),
                pltpu.VMEM(shear.shape, F32),
                dma((dense.shape[0] // 256,)),
                dma((2, chunks)),
                dma((2, chunks)),
                dma((units,)),
                dma((units,)),
                dma((units,)),
                dma((units,)),
                dma((units,)),
                dma((units, rows)),
                dma((units,)),
                dma((units,)),
                dma((units,)),
                dma((units, cols + 1)),
            ],
            compiler_params=pltpu.CompilerParams(
                collective_id=0,
                has_side_effects=True,
                vmem_limit_bytes=62 * 1024 * 1024,
            ),
        )(
            shear,
            state,
            a_param[None, :],
            rate[None, :],
            loading[None, :],
            dense,
            left,
            right,
            admissible,
            ranks,
        )

    wide = P(None, ("row", "col"))
    line = P(("row", "col"))
    placed = (
        wide,
        wide,
        line,
        line,
        line,
        P("row", "col"),
        P("col", "row"),
        P("row", "col"),
        P(),
        P(),
    )
    return jax.shard_map(
        on_device, mesh=mesh, in_specs=placed, out_specs=(wide, wide), check_vma=False
    )
```

```python
import functools
import math

import jax
import jax.numpy as jnp
from jax import lax
from jax.experimental import pallas as pl
from jax.experimental.pallas import tpu as pltpu
from jax.sharding import PartitionSpec as P

TILE = 2048
RANK = 64
GROUP = 16
LAG = 4
LN2 = math.log(2.0)
MESH = pl.DeviceIdType.MESH
F32 = jnp.float32
BF16 = jnp.bfloat16


def kernel(
    rows,
    cols,
    shear_hbm,
    state_hbm,
    a_ref,
    rate_ref,
    load_ref,
    dense_ref,
    left_ref,
    right_ref,
    adm_ref,
    rank_ref,
    shear_out,
    state_out,
    weights,
    gathered,
    vsend,
    staged,
    stage,
    partial,
    psend,
    arrived,
    own,
    shear,
    state,
    k_shear,
    k_state,
    dense_sem,
    in_sem,
    out_sem,
    st_send,
    st_recv,
    p1_send,
    p1_recv,
    p2_send,
    p2_recv,
    sib_send,
    sib_recv,
    rs_send,
    rs_recv,
):
    scenarios, piece = shear.shape
    chunk = rows * GROUP
    chunks = scenarios // chunk
    units = 2 * chunks
    half = rows // 2
    per = rows // cols
    slots = partial.shape[0]
    stages = stage.shape[0]
    r = lax.axis_index("row")
    c = lax.axis_index("col")
    mine = c * per
    sib = r + 1 - 2 * (r % 2)
    sources, targets = weights.shape
    across = sources // TILE
    build_rows = 256
    builds = targets // build_rows
    build_cols = 512
    low = c < cols // 2
    end = (c == 0) | (c == cols - 1)

    def scen(q):
        return pl.ds(pl.multiple_of(q * chunk, chunk), chunk)

    def shear_in(q):
        return pltpu.make_async_copy(
            shear_hbm.at[scen(q), :], shear.at[scen(q), :], in_sem.at[0, q]
        )

    def state_in(q):
        return pltpu.make_async_copy(
            state_hbm.at[scen(q), :], state.at[scen(q), :], in_sem.at[1, q]
        )

    def shear_store(q):
        return pltpu.make_async_copy(
            shear.at[scen(q), :], shear_out.at[scen(q), :], out_sem.at[0, q]
        )

    def state_store(q):
        return pltpu.make_async_copy(
            state.at[scen(q), :], state_out.at[scen(q), :], out_sem.at[1, q]
        )

    def build_order(i):
        if builds % cols:
            return i
        each = builds // cols
        d = jnp.where(low, c + cols - 1 - i // each, c + 1 + i // each) % cols
        return d * each + i % each

    def dense_in(i):
        start = pl.multiple_of(build_order(i) * build_rows, build_rows)
        return pltpu.make_async_copy(
            dense_ref.at[pl.ds(start, build_rows), :],
            stage.at[i % stages],
            dense_sem.at[i],
        )

    def group_of(u, g):
        return gathered.at[u, pl.ds(pl.multiple_of(g * GROUP, GROUP), GROUP), :]

    def part_of(u, g):
        return vsend.at[u, pl.ds(pl.multiple_of(g * GROUP, GROUP), GROUP), :]

    def st_copy(u, j):
        return pltpu.make_async_remote_copy(
            src_ref=part_of(u, j),
            dst_ref=staged.at[u, r],
            send_sem=st_send.at[u],
            recv_sem=st_recv.at[u],
            device_id=(j, c),
            device_id_type=MESH,
        )

    def place(u, source):
        slot = (source % per) * cols + c
        return gathered.at[
            u,
            pl.ds(pl.multiple_of(r * GROUP, GROUP), GROUP),
            pl.ds(pl.multiple_of(slot * piece, piece), piece),
        ]

    def p1_copy(u, source):
        return pltpu.make_async_remote_copy(
            src_ref=staged.at[u, source],
            dst_ref=place(u, source),
            send_sem=p1_send.at[u],
            recv_sem=p1_recv.at[u],
            device_id=(r, source // per),
            device_id_type=MESH,
        )

    def plane_copy(u, g, row_to):
        return pltpu.make_async_remote_copy(
            src_ref=group_of(u, g),
            dst_ref=group_of(u, g),
            send_sem=p2_send.at[u],
            recv_sem=p2_recv.at[u, g],
            device_id=(row_to, c),
            device_id_type=MESH,
        )

    def sib_copy(u, g):
        return pltpu.make_async_remote_copy(
            src_ref=group_of(u, g),
            dst_ref=group_of(u, g),
            send_sem=sib_send.at[u],
            recv_sem=sib_recv.at[u],
            device_id=(sib, c),
            device_id_type=MESH,
        )

    def rs_copy(u, d, to):
        slot = jnp.where(to == d, c, cols + d)
        return pltpu.make_async_remote_copy(
            src_ref=psend.at[u, d],
            dst_ref=arrived.at[u, slot],
            send_sem=rs_send.at[u],
            recv_sem=rs_recv.at[u, slot],
            device_id=(r, to),
            device_id_type=MESH,
        )

    def rs_arrival(u, slot):
        return pltpu.make_async_copy(
            arrived.at[u, slot], arrived.at[u, slot], rs_recv.at[u, slot]
        )

    inv_a = 1.0 / a_ref[...]

    def velocity(shear_now, state_now):
        x = shear_now * inv_a
        fade = jnp.exp(-state_now)
        v = (jnp.exp(x - LN2) - jnp.exp(-x - LN2)) * fade
        return v, rate_ref[...] * (fade - jnp.abs(v))

    def send_slip(u):
        def one(i, _):
            st_copy(u, (r + 1 + i) % rows).start()
            return 0

        lax.fori_loop(0, rows - 1, one, 0)
        pltpu.make_async_copy(part_of(u, r), staged.at[u, r], st_recv.at[u]).start()

    def relay(u):
        pltpu.make_async_copy(staged.at[u], staged.at[u], st_recv.at[u]).wait()

        def one(i, _):
            p1_copy(u, (mine + per + i) % rows).start()
            return 0

        lax.fori_loop(0, rows - per, one, 0)

        def stay(i, _):
            pltpu.make_async_copy(
                staged.at[u, mine + i], place(u, mine + i), p1_recv.at[u]
            ).start()
            return 0

        lax.fori_loop(0, per, stay, 0)

    def first_slip(q, _):
        shear_in(q).wait()
        state_in(q).wait()
        v, ks = velocity(shear[scen(q), :], state[scen(q), :])
        vsend[q] = v.astype(BF16)
        k_state[scen(q), :] = ks
        return 0

    def spread(u):
        pltpu.make_async_copy(group_of(u, r), group_of(u, r), p1_recv.at[u]).wait()

        def one(i, _):
            plane_copy(u, r, (r + 2 * (i + 1)) % rows).start()
            return 0

        lax.fori_loop(0, half - 1, one, 0)
        sib_copy(u, r).start()

    def forward(u):
        def one(i, _):
            g = (r + 2 * (i + 1)) % rows
            plane_copy(u, g, sib).wait_recv()
            sib_copy(u, g).start()
            return 0

        lax.fori_loop(0, half - 1, one, 0)

    def gather_end(u):
        span = pl.ds(0, half * GROUP)
        pltpu.make_async_copy(
            gathered.at[u, span, :], gathered.at[u, span, :], sib_recv.at[u]
        ).wait()

    def multiply(u, i):
        d = jnp.where(low, c + cols - 1 - i, c + 1 + i) % cols
        part = jnp.dot(
            gathered[u],
            weights[:, pl.ds(pl.multiple_of(d * piece, piece), piece)],
            preferred_element_type=F32,
        )
        held = ((c == 1) & (d > c)) | ((c == cols - 2) & (d < c))

        @pl.when(d == c)
        def _():
            own[u % slots] = part

        @pl.when(held)
        def _():
            partial[u % slots, d] = part

        @pl.when((d != c) & jnp.logical_not(held))
        def _():
            psend[u, d] = part.astype(BF16)
            inner = jnp.where(c == 0, 1, cols - 2)
            rs_copy(u, d, jnp.where(end, inner, d)).start()

    def hop(u):
        def one(i, _):
            d = jnp.where(c == 1, cols - 1 - i, i)
            rs_arrival(u, cols + d).wait()
            both = partial[u % slots, d] + arrived[u, cols + d].astype(F32)
            psend[u, d] = both.astype(BF16)
            rs_copy(u, d, d).start()
            return 0

        @pl.when((c == 1) | (c == cols - 2))
        def _():
            lax.fori_loop(0, cols - 2, one, 0)

    def finish(u):
        def one(i, _):
            s = (c + 1 + i) % cols
            inner = (s > 0) & (s < cols - 1)
            beside = ((s == 0) & (c == 1)) | ((s == cols - 1) & (c == cols - 2))

            @pl.when(inner | beside)
            def _():
                rs_arrival(u, s).wait()
                own[u % slots] = own[u % slots] + arrived[u, s].astype(F32)

            return 0

        lax.fori_loop(0, cols - 1, one, 0)

        @pl.when(u < chunks)
        def _():
            here = scen(u)
            ks = load_ref[...] - own[u % slots]
            k_shear[here, :] = ks
            k1 = k_state[here, :]
            old = state[here, :]
            v, k2 = velocity(shear[here, :] + 0.5 * ks, old + 0.5 * k1)
            vsend[u + chunks] = v.astype(BF16)
            send_slip(u + chunks)
            state[here, :] = old + 0.25 * (k1 + k2)
            state_store(u).start()

        @pl.when(u >= chunks)
        def _():
            here = scen(u - chunks)
            ks = load_ref[...] - own[u % slots]
            shear[here, :] = shear[here, :] + 0.25 * (k_shear[here, :] + ks)
            shear_store(u - chunks).start()

    def build(i, _):
        b = build_order(i)
        dense_in(i).wait()
        start = pl.multiple_of(b * build_rows, build_rows)
        here = pl.ds(start, build_rows)
        down = targets // TILE
        td = (b * build_rows) // TILE
        for k in range(across):
            dense = adm_ref[r * down + td, c * across + k]
            rank = rank_ref[r * down + td, c * across + k]
            kept = jnp.where(dense == 1, 0, rank)
            left = left_ref[k * RANK : (k + 1) * RANK, here]
            keep = lax.broadcasted_iota(jnp.int32, (RANK, build_rows), 0) < kept
            left = jnp.where(keep, left.astype(F32), 0.0).astype(BF16)
            scale = jnp.where(dense == 1, 1.0, 0.0).astype(F32)
            scale = jnp.full((build_cols, build_rows), scale, F32).astype(BF16)
            for s in range(TILE // build_cols):
                span = slice(k * TILE + s * build_cols, k * TILE + (s + 1) * build_cols)
                right = right_ref[pl.ds(pl.multiple_of(td * RANK, RANK), RANK), span]
                term = lax.dot_general(
                    right, left, (((0,), (0,)), ((), ())), preferred_element_type=F32
                )
                turned = jnp.transpose(stage[i % stages, :, span])
                weights[span, here] = turned * scale + term.astype(BF16)

        @pl.when(i + stages < builds)
        def _():
            dense_in(i + stages).start()

        return 0

    def drain(u):
        def sent(ref, sem):
            pltpu.make_async_copy(ref, ref, sem).wait()

        sent(vsend.at[u, pl.ds(0, (rows - 1) * GROUP), :], st_send.at[u])
        sent(staged.at[u, pl.ds(0, rows - per)], p1_send.at[u])
        sent(gathered.at[u, pl.ds(0, (half - 1) * GROUP), :], p2_send.at[u])
        sent(gathered.at[u, pl.ds(0, half * GROUP), :], sib_send.at[u])
        sent(psend.at[u, pl.ds(0, cols - 1)], rs_send.at[u])

    barrier = pltpu.get_barrier_semaphore()

    def greet_row(i, _):
        pl.semaphore_signal(
            barrier, inc=1, device_id=((r + 1 + i) % rows, c), device_id_type=MESH
        )
        return 0

    def greet_col(i, _):
        pl.semaphore_signal(
            barrier, inc=1, device_id=(r, (c + 1 + i) % cols), device_id_type=MESH
        )
        return 0

    lax.fori_loop(0, rows - 1, greet_row, 0)
    lax.fori_loop(0, cols - 1, greet_col, 0)

    def fetch(q, _):
        shear_in(q).start()
        state_in(q).start()
        return 0

    lax.fori_loop(0, chunks, fetch, 0)

    def fetch_dense(i, _):
        dense_in(i).start()
        return 0

    lax.fori_loop(0, min(stages, builds), fetch_dense, 0)
    lax.fori_loop(0, chunks, first_slip, 0)
    parts = max(8, chunks + 4)
    cuts = [builds * k // parts for k in range(parts + 1)]

    def build_to(k, n):
        lax.fori_loop(cuts[k], cuts[k + n], build, 0)

    build_to(0, 2)
    pl.semaphore_wait(barrier, rows + cols - 2)

    def first_send(q, _):
        send_slip(q)
        return 0

    lax.fori_loop(0, chunks, first_send, 0)
    build_to(2, 2)
    done = 4
    for q in range(chunks):
        relay(q)
        if q == chunks - 2:
            spread(0)
        build_to(done, 1)
        done += 1
    spread(1)
    build_to(done, parts - done)
    forward(0)

    gap = max(0, LAG - chunks)

    def at_slot(sigma, body, also=True):
        valid = ((sigma >= 0) & (sigma < chunks)) | (
            (sigma >= chunks + gap) & (sigma < units + gap)
        )

        @pl.when(valid & also)
        def _():
            body(jnp.where(sigma < chunks, sigma, sigma - gap))

    def step(t, _):
        at_slot(t, gather_end)

        def one(i, _):
            at_slot(t, lambda u: multiply(u, i))
            return 0

        lax.fori_loop(0, cols, one, 0)
        at_slot(t + 1, forward)
        at_slot(t - 1, finish)
        at_slot(t + 2, spread)
        at_slot(t, hop)
        at_slot(t + 3, relay, t + 3 >= chunks)
        at_slot(t - 3, drain)
        return 0

    lax.fori_loop(0, units + gap + 1, step, 0)

    def last(u, _):
        drain(u)
        return 0

    lax.fori_loop(units - 2, units, last, 0)

    def stored(q, _):
        shear_store(q).wait()
        state_store(q).wait()
        return 0

    lax.fori_loop(0, chunks, stored, 0)


def solution(mesh):
    rows, cols = mesh.shape["row"], mesh.shape["col"]

    def on_device(
        shear, state, a_param, rate, loading, dense, left, right, admissible, ranks
    ):
        scenarios, piece = shear.shape
        chunk = rows * GROUP
        chunks = scenarios // chunk
        units = 2 * chunks
        slots = min(units, 3)
        stages = 6
        vmem = pl.BlockSpec(memory_space=pltpu.VMEM)
        smem = pl.BlockSpec(memory_space=pltpu.SMEM)
        hbm = pl.BlockSpec(memory_space=pl.ANY)
        dma = pltpu.SemaphoreType.DMA
        return pl.pallas_call(
            functools.partial(kernel, rows, cols),
            out_shape=(
                jax.ShapeDtypeStruct(shear.shape, F32),
                jax.ShapeDtypeStruct(shear.shape, F32),
            ),
            in_specs=[hbm] * 2 + [vmem] * 3 + [hbm, vmem, vmem, smem, smem],
            out_specs=(hbm, hbm),
            scratch_shapes=[
                pltpu.VMEM(dense.shape[::-1], BF16),
                pltpu.VMEM((units, chunk, dense.shape[1]), BF16),
                pltpu.VMEM((units, chunk, piece), BF16),
                pltpu.VMEM((units, rows, GROUP, piece), BF16),
                pltpu.VMEM((stages, 256, dense.shape[1]), BF16),
                pltpu.VMEM((slots, cols, chunk, piece), F32),
                pltpu.VMEM((units, cols, chunk, piece), BF16),
                pltpu.VMEM((units, 2 * cols, chunk, piece), BF16),
                pltpu.VMEM((slots, chunk, piece), F32),
                pltpu.VMEM(shear.shape, F32),
                pltpu.VMEM(shear.shape, F32),
                pltpu.VMEM(shear.shape, F32),
                pltpu.VMEM(shear.shape, F32),
                dma((dense.shape[0] // 256,)),
                dma((2, chunks)),
                dma((2, chunks)),
                dma((units,)),
                dma((units,)),
                dma((units,)),
                dma((units,)),
                dma((units,)),
                dma((units, rows)),
                dma((units,)),
                dma((units,)),
                dma((units,)),
                dma((units, 2 * cols)),
            ],
            compiler_params=pltpu.CompilerParams(
                collective_id=0,
                has_side_effects=True,
                vmem_limit_bytes=62 * 1024 * 1024,
            ),
        )(
            shear,
            state,
            a_param[None, :],
            rate[None, :],
            loading[None, :],
            dense,
            left,
            right,
            admissible,
            ranks,
        )

    wide = P(None, ("row", "col"))
    line = P(("row", "col"))
    placed = (
        wide,
        wide,
        line,
        line,
        line,
        P("row", "col"),
        P("col", "row"),
        P("row", "col"),
        P(),
        P(),
    )
    return jax.shard_map(
        on_device, mesh=mesh, in_specs=placed, out_specs=(wide, wide), check_vma=False
    )
```

```python
import functools
import math

import jax
import jax.numpy as jnp
from jax import lax
from jax.experimental import pallas as pl
from jax.experimental.pallas import tpu as pltpu
from jax.sharding import PartitionSpec as P

TILE = 2048
RANK = 64
GROUP = 16
LAG = 4
LN2 = math.log(2.0)
MESH = pl.DeviceIdType.MESH
F32 = jnp.float32
BF16 = jnp.bfloat16


def kernel(
    rows,
    cols,
    shear_hbm,
    state_hbm,
    a_ref,
    rate_ref,
    load_ref,
    dense_ref,
    left_hbm,
    right_hbm,
    adm_ref,
    rank_ref,
    shear,
    state,
    weights,
    gathered,
    vsend,
    staged,
    stage,
    partial,
    psend,
    arrived,
    own,
    k_shear,
    k_state,
    left_ref,
    right_ref,
    dense_sem,
    factor_sem,
    in_sem,
    st_send,
    st_recv,
    p1_send,
    p1_recv,
    p2_send,
    p2_recv,
    sib_send,
    sib_recv,
    rs_send,
    rs_recv,
):
    scenarios, piece = shear.shape
    chunk = rows * GROUP
    chunks = scenarios // chunk
    units = 2 * chunks
    half = rows // 2
    per = rows // cols
    slots = partial.shape[0]
    stages = stage.shape[0]
    r = lax.axis_index("row")
    c = lax.axis_index("col")
    mine = c * per
    sib = r + 1 - 2 * (r % 2)
    sources, targets = weights.shape
    across = sources // TILE
    build_rows = 256
    builds = targets // build_rows
    build_cols = 512
    low = c < cols // 2

    def scen(q):
        return pl.ds(pl.multiple_of(q * chunk, chunk), chunk)

    def shear_in(q):
        return pltpu.make_async_copy(
            shear_hbm.at[scen(q), :], shear.at[scen(q), :], in_sem.at[0, q]
        )

    def state_in(q):
        return pltpu.make_async_copy(
            state_hbm.at[scen(q), :], state.at[scen(q), :], in_sem.at[1, q]
        )

    def build_order(i):
        if builds % cols:
            return i
        each = builds // cols
        d = jnp.where(low, c + cols - 1 - i // each, c + 1 + i // each) % cols
        return d * each + i % each

    def dense_in(i):
        start = pl.multiple_of(build_order(i) * build_rows, build_rows)
        return pltpu.make_async_copy(
            dense_ref.at[pl.ds(start, build_rows), :],
            stage.at[i % stages],
            dense_sem.at[i],
        )

    def group_of(u, g):
        return gathered.at[u, pl.ds(pl.multiple_of(g * GROUP, GROUP), GROUP), :]

    def part_of(u, g):
        return vsend.at[u, pl.ds(pl.multiple_of(g * GROUP, GROUP), GROUP), :]

    def st_copy(u, j):
        return pltpu.make_async_remote_copy(
            src_ref=part_of(u, j),
            dst_ref=staged.at[u, r],
            send_sem=st_send.at[u],
            recv_sem=st_recv.at[u],
            device_id=(j, c),
            device_id_type=MESH,
        )

    def place(u, source):
        slot = (source % per) * cols + c
        return gathered.at[
            u,
            pl.ds(pl.multiple_of(r * GROUP, GROUP), GROUP),
            pl.ds(pl.multiple_of(slot * piece, piece), piece),
        ]

    def p1_copy(u, source):
        return pltpu.make_async_remote_copy(
            src_ref=staged.at[u, source],
            dst_ref=place(u, source),
            send_sem=p1_send.at[u],
            recv_sem=p1_recv.at[u],
            device_id=(r, source // per),
            device_id_type=MESH,
        )

    def plane_copy(u, g, row_to):
        return pltpu.make_async_remote_copy(
            src_ref=group_of(u, g),
            dst_ref=group_of(u, g),
            send_sem=p2_send.at[u],
            recv_sem=p2_recv.at[u, g],
            device_id=(row_to, c),
            device_id_type=MESH,
        )

    def sib_copy(u, g):
        return pltpu.make_async_remote_copy(
            src_ref=group_of(u, g),
            dst_ref=group_of(u, g),
            send_sem=sib_send.at[u],
            recv_sem=sib_recv.at[u, g // 2],
            device_id=(sib, c),
            device_id_type=MESH,
        )

    def rs_copy(u, d, to, span):
        slot = jnp.where(to == d, c, cols + d)
        return pltpu.make_async_remote_copy(
            src_ref=psend.at[u, d, span],
            dst_ref=arrived.at[u, slot, span],
            send_sem=rs_send.at[u],
            recv_sem=rs_recv.at[u, slot],
            device_id=(r, to),
            device_id_type=MESH,
        )

    def rs_arrival(u, slot):
        return pltpu.make_async_copy(
            arrived.at[u, slot], arrived.at[u, slot], rs_recv.at[u, slot]
        )

    inv_a = 1.0 / a_ref[...]

    def velocity(shear_now, state_now):
        x = shear_now * inv_a
        fade = jnp.exp(-state_now)
        v = (jnp.exp(x - LN2) - jnp.exp(-x - LN2)) * fade
        return v, rate_ref[...] * (fade - jnp.abs(v))

    def send_slip(u):
        def one(i, _):
            st_copy(u, (r + 1 + i) % rows).start()
            return 0

        lax.fori_loop(0, rows - 1, one, 0)
        pltpu.make_async_copy(part_of(u, r), staged.at[u, r], st_recv.at[u]).start()

    def relay(u):
        pltpu.make_async_copy(staged.at[u], staged.at[u], st_recv.at[u]).wait()

        def one(i, _):
            p1_copy(u, (mine + per + i) % rows).start()
            return 0

        lax.fori_loop(0, rows - per, one, 0)

        def stay(i, _):
            pltpu.make_async_copy(
                staged.at[u, mine + i], place(u, mine + i), p1_recv.at[u]
            ).start()
            return 0

        lax.fori_loop(0, per, stay, 0)

    def first_slip(q, _):
        shear_in(q).wait()
        state_in(q).wait()
        v, ks = velocity(shear[scen(q), :], state[scen(q), :])
        vsend[q] = v.astype(BF16)
        k_state[scen(q), :] = ks
        return 0

    first_row = (r // half) * half

    def peer(i):
        inside = half // 2 - 1
        near = first_row + (r - first_row + 2 * (i + 1)) % half
        across_rows = (first_row + half) % rows + (r - first_row + 2 * (i - inside)) % half
        return jnp.where(i < inside, near, across_rows)

    def spread(u):
        pltpu.make_async_copy(group_of(u, r), group_of(u, r), p1_recv.at[u]).wait()

        def one(i, _):
            plane_copy(u, r, peer(i)).start()
            return 0

        lax.fori_loop(0, half - 1, one, 0)
        sib_copy(u, r).start()

    def forward_from(u, first, last):
        def one(i, _):
            plane_copy(u, peer(i), sib).wait_recv()
            sib_copy(u, peer(i)).start()
            return 0

        lax.fori_loop(first, last, one, 0)

    def forward(u):
        forward_from(u, 0, half - 1)

    def arrive(u, first, last):
        def one(i, _):
            g = (first_row + 2 * i + sib % 2) % rows
            sib_copy(u, g).wait_recv()
            return 0

        lax.fori_loop(first, last, one, 0)

    def gather_end(u):
        arrive(u, 0, half)

    def multiply(u, i, span=slice(None)):
        d = jnp.where(low, c + cols - 1 - i, c + 1 + i) % cols
        part = jnp.dot(
            gathered[u, span],
            weights[:, pl.ds(pl.multiple_of(d * piece, piece), piece)],
            preferred_element_type=F32,
        )
        held = ((c == 1) & (d > c)) | ((c == cols - 2) & (d < c))

        @pl.when(d == c)
        def _():
            own[u % slots, span] = part

        @pl.when(held)
        def _():
            partial[u % slots, d, span] = part

        @pl.when((d != c) & jnp.logical_not(held))
        def _():
            psend[u, d, span] = part.astype(BF16)
            to = jnp.where(c == 0, 1, jnp.where(c == cols - 1, cols - 2, d))
            rs_copy(u, d, to, span).start()

    def hop(u):
        def one(i, _):
            d = jnp.where(c == 1, cols - 1 - i, i)
            rs_arrival(u, cols + d).wait()
            both = partial[u % slots, d] + arrived[u, cols + d].astype(F32)
            psend[u, d] = both.astype(BF16)
            rs_copy(u, d, d, slice(None)).start()
            return 0

        @pl.when((c == 1) | (c == cols - 2))
        def _():
            lax.fori_loop(0, cols - 2, one, 0)

    def finish(u):
        def one(i, _):
            s = (c + 1 + i) % cols
            inner = (s > 0) & (s < cols - 1)
            beside = ((s == 0) & (c == 1)) | ((s == cols - 1) & (c == cols - 2))

            @pl.when(inner | beside)
            def _():
                rs_arrival(u, s).wait()
                own[u % slots] = own[u % slots] + arrived[u, s].astype(F32)

            return 0

        lax.fori_loop(0, cols - 1, one, 0)

        @pl.when(u < chunks)
        def _():
            here = scen(u)
            ks = load_ref[...] - own[u % slots]
            k_shear[here, :] = ks
            k1 = k_state[here, :]
            old = state[here, :]
            v, k2 = velocity(shear[here, :] + 0.5 * ks, old + 0.5 * k1)
            vsend[u + chunks] = v.astype(BF16)
            send_slip(u + chunks)
            state[here, :] = old + 0.25 * (k1 + k2)

        @pl.when(u >= chunks)
        def _():
            here = scen(u - chunks)
            ks = load_ref[...] - own[u % slots]
            shear[here, :] = shear[here, :] + 0.25 * (k_shear[here, :] + ks)

    def build(i, _):
        b = build_order(i)
        dense_in(i).wait()
        start = pl.multiple_of(b * build_rows, build_rows)
        here = pl.ds(start, build_rows)
        down = targets // TILE
        td = (b * build_rows) // TILE
        for k in range(across):
            dense = adm_ref[r * down + td, c * across + k]
            rank = rank_ref[r * down + td, c * across + k]
            kept = jnp.where(dense == 1, 0, rank)
            left = left_ref[k * RANK : (k + 1) * RANK, here]
            keep = lax.broadcasted_iota(jnp.int32, (RANK, build_rows), 0) < kept
            left = jnp.where(keep, left.astype(F32), 0.0).astype(BF16)
            scale = jnp.where(dense == 1, 1.0, 0.0).astype(F32)
            scale = jnp.full((build_cols, build_rows), scale, F32).astype(BF16)
            for s in range(TILE // build_cols):
                span = slice(k * TILE + s * build_cols, k * TILE + (s + 1) * build_cols)
                right = right_ref[pl.ds(pl.multiple_of(td * RANK, RANK), RANK), span]
                term = lax.dot_general(
                    right, left, (((0,), (0,)), ((), ())), preferred_element_type=F32
                )
                turned = jnp.transpose(stage[i % stages, :, span])
                weights[span, here] = turned * scale + term.astype(BF16)

        @pl.when(i + stages < builds)
        def _():
            dense_in(i + stages).start()

        return 0

    def drain(u):
        def sent(ref, sem):
            pltpu.make_async_copy(ref, ref, sem).wait()

        sent(vsend.at[u, pl.ds(0, (rows - 1) * GROUP), :], st_send.at[u])
        sent(staged.at[u, pl.ds(0, rows - per)], p1_send.at[u])
        sent(gathered.at[u, pl.ds(0, (half - 1) * GROUP), :], p2_send.at[u])
        sent(gathered.at[u, pl.ds(0, half * GROUP), :], sib_send.at[u])
        sent(psend.at[u, pl.ds(0, cols - 1)], rs_send.at[u])

    barrier = pltpu.get_barrier_semaphore()

    def greet_row(i, _):
        pl.semaphore_signal(
            barrier, inc=1, device_id=((r + 1 + i) % rows, c), device_id_type=MESH
        )
        return 0

    def greet_col(i, _):
        pl.semaphore_signal(
            barrier, inc=1, device_id=(r, (c + 1 + i) % cols), device_id_type=MESH
        )
        return 0

    lax.fori_loop(0, rows - 1, greet_row, 0)
    lax.fori_loop(0, cols - 1, greet_col, 0)

    def fetch(q, _):
        shear_in(q).start()
        state_in(q).start()
        return 0

    lax.fori_loop(0, chunks, fetch, 0)
    left_in = pltpu.make_async_copy(left_hbm, left_ref, factor_sem.at[0])
    right_in = pltpu.make_async_copy(right_hbm, right_ref, factor_sem.at[1])
    left_in.start()
    right_in.start()

    def fetch_dense(i, _):
        dense_in(i).start()
        return 0

    lax.fori_loop(0, min(stages, builds), fetch_dense, 0)
    lax.fori_loop(0, chunks, first_slip, 0)
    parts = max(8, chunks + 4)
    cuts = [builds * k // parts for k in range(parts + 1)]

    def build_to(k, n):
        lax.fori_loop(cuts[k], cuts[k + n], build, 0)

    left_in.wait()
    right_in.wait()
    build_to(0, 2)
    pl.semaphore_wait(barrier, rows + cols - 2)

    def first_send(q, _):
        send_slip(q)
        return 0

    lax.fori_loop(0, chunks, first_send, 0)
    build_to(2, 2)
    done = 4
    for q in range(chunks):
        relay(q)
        if q == chunks - 2:
            spread(0)
        build_to(done, 1)
        done += 1
    spread(1)
    build_to(done, parts - done)
    rows_half = chunk // 2

    def unit_half(row):
        return pl.ds(pl.multiple_of(row * GROUP, rows_half), rows_half)

    upper = unit_half(first_row)
    lower = unit_half((first_row + half) % rows)
    inside = half // 2 - 1
    forward_from(0, 0, inside)
    arrive(0, 0, half // 2)

    def first_half(i, _):
        multiply(0, i, upper)

        @pl.when(i == 0)
        def _():
            forward_from(0, inside, half - 2)

        return 0

    def second_half(i, _):
        multiply(0, i, lower)
        return 0

    lax.fori_loop(0, cols - 2, first_half, 0)
    forward_from(0, half - 2, half - 1)
    arrive(0, half // 2, half)
    lax.fori_loop(0, cols - 2, second_half, 0)

    gap = max(0, LAG - chunks)

    def at_slot(sigma, body, also=True):
        valid = ((sigma >= 0) & (sigma < chunks)) | (
            (sigma >= chunks + gap) & (sigma < units + gap)
        )

        @pl.when(valid & also)
        def _():
            body(jnp.where(sigma < chunks, sigma, sigma - gap))

    def step(t, _):
        def one(i, _):
            at_slot(t, lambda u: multiply(u, i), (t > 0) | (i >= cols - 2))
            return 0

        lax.fori_loop(1, cols, one, 0)
        at_slot(t + 1, forward)
        at_slot(t - 1, finish)
        at_slot(t + 2, spread)
        at_slot(t, hop)
        at_slot(t + 1, gather_end)
        at_slot(t + 1, lambda u: multiply(u, 0))
        at_slot(t + 3, relay, t + 3 >= chunks)
        at_slot(t - 3, drain)
        return 0

    lax.fori_loop(0, units + gap + 1, step, 0)

    def last(u, _):
        drain(u)
        return 0

    lax.fori_loop(units - 2, units, last, 0)


def hand_over(shear, state, shear_out, state_out, sem):
    first = pltpu.make_async_copy(shear, shear_out, sem.at[0])
    second = pltpu.make_async_copy(state, state_out, sem.at[1])
    first.start()
    second.start()
    first.wait()
    second.wait()


def solution(mesh):
    rows, cols = mesh.shape["row"], mesh.shape["col"]

    def on_device(
        shear, state, a_param, rate, loading, dense, left, right, admissible, ranks
    ):
        scenarios, piece = shear.shape
        chunk = rows * GROUP
        chunks = scenarios // chunk
        units = 2 * chunks
        slots = min(units, 3)
        half = rows // 2
        stages = 4
        vmem = pl.BlockSpec(memory_space=pltpu.VMEM)
        smem = pl.BlockSpec(memory_space=pltpu.SMEM)
        hbm = pl.BlockSpec(memory_space=pl.ANY)
        dma = pltpu.SemaphoreType.DMA
        after = pl.pallas_call(
            functools.partial(kernel, rows, cols),
            out_shape=(pltpu.VMEM(shear.shape, F32), pltpu.VMEM(shear.shape, F32)),
            in_specs=[hbm] * 2 + [vmem] * 3 + [hbm] * 3 + [smem] * 2,
            out_specs=(vmem, vmem),
            scratch_shapes=[
                pltpu.VMEM(dense.shape[::-1], BF16),
                pltpu.VMEM((units, chunk, dense.shape[1]), BF16),
                pltpu.VMEM((units, chunk, piece), BF16),
                pltpu.VMEM((units, rows, GROUP, piece), BF16),
                pltpu.VMEM((stages, 256, dense.shape[1]), BF16),
                pltpu.VMEM((slots, cols, chunk, piece), F32),
                pltpu.VMEM((units, cols, chunk, piece), BF16),
                pltpu.VMEM((units, 2 * cols, chunk, piece), BF16),
                pltpu.VMEM((slots, chunk, piece), F32),
                pltpu.VMEM(shear.shape, F32),
                pltpu.VMEM(shear.shape, F32),
                pltpu.VMEM(left.shape, BF16),
                pltpu.VMEM(right.shape, BF16),
                dma((dense.shape[0] // 256,)),
                dma((2,)),
                dma((2, chunks)),
                dma((units,)),
                dma((units,)),
                dma((units,)),
                dma((units,)),
                dma((units,)),
                dma((units, rows)),
                dma((units,)),
                dma((units, half)),
                dma((units,)),
                dma((units, 2 * cols)),
            ],
            compiler_params=pltpu.CompilerParams(
                collective_id=0,
                has_side_effects=True,
                vmem_limit_bytes=57 * 1024 * 1024,
            ),
        )(
            shear,
            state,
            a_param[None, :],
            rate[None, :],
            loading[None, :],
            dense,
            left,
            right,
            admissible,
            ranks,
        )
        return pl.pallas_call(
            hand_over,
            out_shape=(
                jax.ShapeDtypeStruct(shear.shape, F32),
                jax.ShapeDtypeStruct(shear.shape, F32),
            ),
            in_specs=[vmem] * 2,
            out_specs=(hbm, hbm),
            scratch_shapes=[dma((2,))],
            compiler_params=pltpu.CompilerParams(vmem_limit_bytes=4 * 1024 * 1024),
        )(*after)

    wide = P(None, ("row", "col"))
    line = P(("row", "col"))
    placed = (
        wide,
        wide,
        line,
        line,
        line,
        P("row", "col"),
        P("col", "row"),
        P("row", "col"),
        P(),
        P(),
    )
    return jax.shard_map(
        on_device, mesh=mesh, in_specs=placed, out_specs=(wide, wide), check_vma=False
    )
```

```python
import functools
import math

import jax
import jax.numpy as jnp
from jax import lax
from jax.experimental import pallas as pl
from jax.experimental.pallas import tpu as pltpu
from jax.sharding import PartitionSpec as P

TILE = 2048
RANK = 64
GROUP = 16
LAG = 4
LN2 = math.log(2.0)
MESH = pl.DeviceIdType.MESH
F32 = jnp.float32
BF16 = jnp.bfloat16


def kernel(
    rows,
    cols,
    shear_hbm,
    state_hbm,
    a_hbm,
    rate_hbm,
    load_hbm,
    dense_ref,
    left_hbm,
    right_hbm,
    adm_hbm,
    rank_hbm,
    shear,
    state,
    weights,
    gathered,
    vsend,
    staged,
    stage,
    partial,
    psend,
    arrived,
    own,
    k_shear,
    k_state,
    left_ref,
    right_ref,
    a_ref,
    rate_ref,
    load_ref,
    adm_ref,
    rank_ref,
    dense_sem,
    small_sem,
    in_sem,
    st_send,
    st_recv,
    p1_send,
    p1_recv,
    p2_send,
    p2_recv,
    sib_send,
    sib_recv,
    rs_send,
    rs_recv,
):
    scenarios, piece = shear.shape
    chunk = rows * GROUP
    chunks = scenarios // chunk
    units = 2 * chunks
    half = rows // 2
    per = rows // cols
    slots = partial.shape[0]
    stages = stage.shape[0]
    r = lax.axis_index("row")
    c = lax.axis_index("col")
    mine = c * per
    sib = r + 1 - 2 * (r % 2)
    sources, targets = weights.shape
    across = sources // TILE
    build_rows = 256
    builds = targets // build_rows
    build_cols = 512
    low = c < cols // 2

    def scen(q):
        return pl.ds(pl.multiple_of(q * chunk, chunk), chunk)

    def shear_in(q):
        return pltpu.make_async_copy(
            shear_hbm.at[scen(q), :], shear.at[scen(q), :], in_sem.at[0, q]
        )

    def state_in(q):
        return pltpu.make_async_copy(
            state_hbm.at[scen(q), :], state.at[scen(q), :], in_sem.at[1, q]
        )

    def build_order(i):
        if builds % cols:
            return i
        each = builds // cols
        d = jnp.where(low, c + cols - 1 - i // each, c + 1 + i // each) % cols
        return d * each + i % each

    def dense_in(i):
        start = pl.multiple_of(build_order(i) * build_rows, build_rows)
        return pltpu.make_async_copy(
            dense_ref.at[pl.ds(start, build_rows), :],
            stage.at[i % stages],
            dense_sem.at[i],
        )

    def group_of(u, g):
        return gathered.at[u, pl.ds(pl.multiple_of(g * GROUP, GROUP), GROUP), :]

    def part_of(u, g):
        return vsend.at[u, pl.ds(pl.multiple_of(g * GROUP, GROUP), GROUP), :]

    def st_copy(u, j):
        return pltpu.make_async_remote_copy(
            src_ref=part_of(u, j),
            dst_ref=staged.at[u, r],
            send_sem=st_send.at[u],
            recv_sem=st_recv.at[u % chunks],
            device_id=(j, c),
            device_id_type=MESH,
        )

    def place(u, source):
        slot = (source % per) * cols + c
        return gathered.at[
            u,
            pl.ds(pl.multiple_of(r * GROUP, GROUP), GROUP),
            pl.ds(pl.multiple_of(slot * piece, piece), piece),
        ]

    def p1_copy(u, source):
        return pltpu.make_async_remote_copy(
            src_ref=staged.at[u, source],
            dst_ref=place(u, source),
            send_sem=p1_send.at[u],
            recv_sem=p1_recv.at[u % chunks],
            device_id=(r, source // per),
            device_id_type=MESH,
        )

    def plane_copy(u, g, row_to):
        return pltpu.make_async_remote_copy(
            src_ref=group_of(u, g),
            dst_ref=group_of(u, g),
            send_sem=p2_send.at[u],
            recv_sem=p2_recv.at[u % chunks, g // 2],
            device_id=(row_to, c),
            device_id_type=MESH,
        )

    def sib_copy(u, g):
        return pltpu.make_async_remote_copy(
            src_ref=group_of(u, g),
            dst_ref=group_of(u, g),
            send_sem=sib_send.at[u],
            recv_sem=sib_recv.at[u % chunks, g // 2],
            device_id=(sib, c),
            device_id_type=MESH,
        )

    def rs_copy(u, d, to, span):
        slot = jnp.where(to == d, c, cols + d)
        return pltpu.make_async_remote_copy(
            src_ref=psend.at[u, d, span],
            dst_ref=arrived.at[u, slot, span],
            send_sem=rs_send.at[u],
            recv_sem=rs_recv.at[u % chunks, slot],
            device_id=(r, to),
            device_id_type=MESH,
        )

    def rs_arrival(u, slot):
        return pltpu.make_async_copy(
            arrived.at[u, slot], arrived.at[u, slot], rs_recv.at[u % chunks, slot]
        )

    def velocity(shear_now, state_now):
        x = shear_now * a_ref[...]
        fade = jnp.exp(-state_now)
        v = (jnp.exp(x - LN2) - jnp.exp(-x - LN2)) * fade
        return v, rate_ref[...] * (fade - jnp.abs(v))

    def send_slip(u):
        def one(i, _):
            st_copy(u, (r + 1 + i) % rows).start()
            return 0

        lax.fori_loop(0, rows - 1, one, 0)
        pltpu.make_async_copy(part_of(u, r), staged.at[u, r], st_recv.at[u % chunks]).start()

    def relay(u):
        pltpu.make_async_copy(staged.at[u], staged.at[u], st_recv.at[u % chunks]).wait()

        def one(i, _):
            p1_copy(u, (mine + per + i) % rows).start()
            return 0

        lax.fori_loop(0, rows - per, one, 0)

        def stay(i, _):
            pltpu.make_async_copy(
                staged.at[u, mine + i], place(u, mine + i), p1_recv.at[u % chunks]
            ).start()
            return 0

        lax.fori_loop(0, per, stay, 0)

    def first_slip(q, _):
        shear_in(q).wait()
        state_in(q).wait()
        v, ks = velocity(shear[scen(q), :], state[scen(q), :])
        vsend[q] = v.astype(BF16)
        k_state[scen(q), :] = ks
        return 0

    first_row = (r // half) * half

    def peer(i):
        inside = half // 2 - 1
        near = first_row + (r - first_row + 2 * (i + 1)) % half
        across_rows = (first_row + half) % rows + (r - first_row + 2 * (i - inside)) % half
        return jnp.where(i < inside, near, across_rows)

    def spread(u):
        pltpu.make_async_copy(group_of(u, r), group_of(u, r), p1_recv.at[u % chunks]).wait()

        def one(i, _):
            plane_copy(u, r, peer(i)).start()
            return 0

        lax.fori_loop(0, half - 1, one, 0)
        sib_copy(u, r).start()

    def forward_from(u, first, last):
        def one(i, _):
            plane_copy(u, peer(i), sib).wait_recv()
            sib_copy(u, peer(i)).start()
            return 0

        lax.fori_loop(first, last, one, 0)

    def forward(u):
        forward_from(u, 0, half - 1)

    def arrive(u, first, last):
        def one(i, _):
            g = (first_row + 2 * i + sib % 2) % rows
            sib_copy(u, g).wait_recv()
            return 0

        lax.fori_loop(first, last, one, 0)

    def gather_end(u):
        arrive(u, 0, half)

    def multiply(u, i, span=slice(None)):
        d = jnp.where(low, c + cols - 1 - i, c + 1 + i) % cols
        part = jnp.dot(
            gathered[u, span],
            weights[:, pl.ds(pl.multiple_of(d * piece, piece), piece)],
            preferred_element_type=F32,
        )
        held = ((c == 1) & (d > c)) | ((c == cols - 2) & (d < c))

        @pl.when(d == c)
        def _():
            own[u % slots, span] = part

        @pl.when(held)
        def _():
            partial[u % slots, d, span] = part

        @pl.when((d != c) & jnp.logical_not(held))
        def _():
            psend[u, d, span] = part.astype(BF16)
            to = jnp.where(c == 0, 1, jnp.where(c == cols - 1, cols - 2, d))
            rs_copy(u, d, to, span).start()

    def hop(u):
        def one(i, _):
            d = jnp.where(c == 1, cols - 1 - i, i)
            rs_arrival(u, cols + d).wait()
            both = partial[u % slots, d] + arrived[u, cols + d].astype(F32)
            psend[u, d] = both.astype(BF16)
            rs_copy(u, d, d, slice(None)).start()
            return 0

        @pl.when((c == 1) | (c == cols - 2))
        def _():
            lax.fori_loop(0, cols - 2, one, 0)

    def finish(u):
        def one(i, _):
            s = (c + 1 + i) % cols
            inner = (s > 0) & (s < cols - 1)
            beside = ((s == 0) & (c == 1)) | ((s == cols - 1) & (c == cols - 2))

            @pl.when(inner | beside)
            def _():
                rs_arrival(u, s).wait()
                own[u % slots] = own[u % slots] + arrived[u, s].astype(F32)

            return 0

        lax.fori_loop(0, cols - 1, one, 0)

        @pl.when(u < chunks)
        def _():
            here = scen(u)
            ks = load_ref[...] - own[u % slots]
            k_shear[here, :] = ks
            k1 = k_state[here, :]
            old = state[here, :]
            v, k2 = velocity(shear[here, :] + 0.5 * ks, old + 0.5 * k1)
            vsend[u + chunks] = v.astype(BF16)
            send_slip(u + chunks)
            state[here, :] = old + 0.25 * (k1 + k2)

        @pl.when(u >= chunks)
        def _():
            here = scen(u - chunks)
            ks = load_ref[...] - own[u % slots]
            shear[here, :] = shear[here, :] + 0.25 * (k_shear[here, :] + ks)

    def build(i, _):
        b = build_order(i)
        dense_in(i).wait()
        start = pl.multiple_of(b * build_rows, build_rows)
        here = pl.ds(start, build_rows)
        down = targets // TILE
        td = (b * build_rows) // TILE
        for k in range(across):
            dense = adm_ref[r * down + td, c * across + k]
            rank = rank_ref[r * down + td, c * across + k]
            kept = jnp.where(dense == 1, 0, rank)
            left = left_ref[k * RANK : (k + 1) * RANK, here]
            keep = lax.broadcasted_iota(jnp.int32, (RANK, build_rows), 0) < kept
            left = jnp.where(keep, left.astype(F32), 0.0).astype(BF16)
            scale = jnp.where(dense == 1, 1.0, 0.0).astype(F32)
            scale = jnp.full((build_cols, build_rows), scale, F32).astype(BF16)
            for s in range(TILE // build_cols):
                span = slice(k * TILE + s * build_cols, k * TILE + (s + 1) * build_cols)
                right = right_ref[pl.ds(pl.multiple_of(td * RANK, RANK), RANK), span]
                term = lax.dot_general(
                    right, left, (((0,), (0,)), ((), ())), preferred_element_type=F32
                )
                turned = jnp.transpose(stage[i % stages, :, span])
                weights[span, here] = turned * scale + term.astype(BF16)

        @pl.when(i + stages < builds)
        def _():
            dense_in(i + stages).start()

        return 0

    def drain(u):
        def sent(ref, sem):
            pltpu.make_async_copy(ref, ref, sem).wait()

        sent(vsend.at[u, pl.ds(0, (rows - 1) * GROUP), :], st_send.at[u])
        sent(staged.at[u, pl.ds(0, rows - per)], p1_send.at[u])
        sent(gathered.at[u, pl.ds(0, (half - 1) * GROUP), :], p2_send.at[u])
        sent(gathered.at[u, pl.ds(0, half * GROUP), :], sib_send.at[u])
        sent(psend.at[u, pl.ds(0, cols - 1)], rs_send.at[u])

    barrier = pltpu.get_barrier_semaphore()

    def greet_row(i, _):
        pl.semaphore_signal(
            barrier, inc=1, device_id=((r + 1 + i) % rows, c), device_id_type=MESH
        )
        return 0

    def greet_col(i, _):
        pl.semaphore_signal(
            barrier, inc=1, device_id=(r, (c + 1 + i) % cols), device_id_type=MESH
        )
        return 0

    lax.fori_loop(0, rows - 1, greet_row, 0)
    lax.fori_loop(0, cols - 1, greet_col, 0)

    small = [
        pltpu.make_async_copy(src, dst, small_sem.at[k])
        for k, (src, dst) in enumerate(
            (
                (a_hbm, a_ref),
                (rate_hbm, rate_ref),
                (load_hbm, load_ref),
                (adm_hbm, adm_ref),
                (rank_hbm, rank_ref),
                (left_hbm, left_ref),
                (right_hbm, right_ref),
            )
        )
    ]
    for copy in small:
        copy.start()

    def fetch(q, _):
        shear_in(q).start()
        state_in(q).start()
        return 0

    lax.fori_loop(0, chunks, fetch, 0)

    def fetch_dense(i, _):
        dense_in(i).start()
        return 0

    lax.fori_loop(0, min(stages, builds), fetch_dense, 0)
    for copy in small[:3]:
        copy.wait()
    a_ref[...] = 1.0 / a_ref[...]
    lax.fori_loop(0, 1, first_slip, 0)
    parts = max(8, chunks + 4)
    cuts = [builds * k // parts for k in range(parts + 1)]

    def build_to(k, n):
        lax.fori_loop(cuts[k], cuts[k + n], build, 0)

    for copy in small[3:]:
        copy.wait()
    pl.semaphore_wait(barrier, rows + cols - 2)

    def first_send(q, _):
        send_slip(q)
        return 0

    first_send(0, 0)
    lax.fori_loop(1, chunks, first_slip, 0)
    lax.fori_loop(1, chunks, first_send, 0)
    build_to(0, 2)
    done = 2
    for q in range(chunks):
        relay(q)
        if q == chunks - 2:
            spread(0)
        build_to(done, 1)
        done += 1
    spread(1)
    build_to(done, parts - done)
    rows_half = chunk // 2

    def unit_half(row):
        return pl.ds(pl.multiple_of(row * GROUP, rows_half), rows_half)

    upper = unit_half(first_row)
    lower = unit_half((first_row + half) % rows)
    inside = half // 2 - 1
    forward_from(0, 0, inside)
    arrive(0, 0, half // 2)

    def first_half(i, _):
        multiply(0, i, upper)

        @pl.when(i == 0)
        def _():
            forward_from(0, inside, half - 2)

        return 0

    def second_half(i, _):
        multiply(0, i, lower)
        return 0

    lax.fori_loop(0, cols - 2, first_half, 0)
    forward_from(0, half - 2, half - 1)
    arrive(0, half // 2, half)
    lax.fori_loop(0, cols - 2, second_half, 0)

    gap = max(0, LAG - chunks)

    def at_slot(sigma, body, also=True):
        valid = ((sigma >= 0) & (sigma < chunks)) | (
            (sigma >= chunks + gap) & (sigma < units + gap)
        )

        @pl.when(valid & also)
        def _():
            body(jnp.where(sigma < chunks, sigma, sigma - gap))

    def step(t, _):
        def one(i, _):
            at_slot(t, lambda u: multiply(u, i), (t > 0) | (i >= cols - 2))
            return 0

        lax.fori_loop(1, cols, one, 0)
        at_slot(t + 1, forward)
        at_slot(t - 1, finish)
        at_slot(t + 2, spread)
        at_slot(t, hop)
        at_slot(t + 1, gather_end)
        at_slot(t + 1, lambda u: multiply(u, 0))
        at_slot(t + 3, relay, t + 3 >= chunks)
        at_slot(t - 3, drain)
        return 0

    lax.fori_loop(0, units + gap + 1, step, 0)

    def last(u, _):
        drain(u)
        return 0

    lax.fori_loop(units - 2, units, last, 0)


def hand_over(shear, state, shear_out, state_out, sem):
    first = pltpu.make_async_copy(shear, shear_out, sem.at[0])
    second = pltpu.make_async_copy(state, state_out, sem.at[1])
    first.start()
    second.start()
    first.wait()
    second.wait()


def solution(mesh):
    rows, cols = mesh.shape["row"], mesh.shape["col"]

    def on_device(
        shear, state, a_param, rate, loading, dense, left, right, admissible, ranks
    ):
        scenarios, piece = shear.shape
        chunk = rows * GROUP
        chunks = scenarios // chunk
        units = 2 * chunks
        slots = min(units, 3)
        half = rows // 2
        stages = 4
        vmem = pl.BlockSpec(memory_space=pltpu.VMEM)
        hbm = pl.BlockSpec(memory_space=pl.ANY)
        dma = pltpu.SemaphoreType.DMA
        after = pl.pallas_call(
            functools.partial(kernel, rows, cols),
            out_shape=(pltpu.VMEM(shear.shape, F32), pltpu.VMEM(shear.shape, F32)),
            in_specs=[hbm] * 10,
            out_specs=(vmem, vmem),
            scratch_shapes=[
                pltpu.VMEM(dense.shape[::-1], BF16),
                pltpu.VMEM((units, chunk, dense.shape[1]), BF16),
                pltpu.VMEM((units, chunk, piece), BF16),
                pltpu.VMEM((units, rows, GROUP, piece), BF16),
                pltpu.VMEM((stages, 256, dense.shape[1]), BF16),
                pltpu.VMEM((slots, cols, chunk, piece), F32),
                pltpu.VMEM((units, cols, chunk, piece), BF16),
                pltpu.VMEM((units, 2 * cols, chunk, piece), BF16),
                pltpu.VMEM((slots, chunk, piece), F32),
                pltpu.VMEM(shear.shape, F32),
                pltpu.VMEM(shear.shape, F32),
                pltpu.VMEM(left.shape, BF16),
                pltpu.VMEM(right.shape, BF16),
                pltpu.VMEM((1, piece), F32),
                pltpu.VMEM((1, piece), F32),
                pltpu.VMEM((1, piece), F32),
                pltpu.SMEM(admissible.shape, jnp.int32),
                pltpu.SMEM(ranks.shape, jnp.int32),
                dma((dense.shape[0] // 256,)),
                dma((7,)),
                dma((2, chunks)),
                dma((units,)),
                dma((chunks,)),
                dma((units,)),
                dma((chunks,)),
                dma((units,)),
                dma((chunks, half)),
                dma((units,)),
                dma((chunks, half)),
                dma((units,)),
                dma((chunks, 2 * cols)),
            ],
            compiler_params=pltpu.CompilerParams(
                collective_id=0,
                has_side_effects=True,
                vmem_limit_bytes=57 * 1024 * 1024,
            ),
        )(
            shear,
            state,
            a_param[None, :],
            rate[None, :],
            loading[None, :],
            dense,
            left,
            right,
            admissible,
            ranks,
        )
        return pl.pallas_call(
            hand_over,
            out_shape=(
                jax.ShapeDtypeStruct(shear.shape, F32),
                jax.ShapeDtypeStruct(shear.shape, F32),
            ),
            in_specs=[vmem] * 2,
            out_specs=(hbm, hbm),
            scratch_shapes=[dma((2,))],
            compiler_params=pltpu.CompilerParams(vmem_limit_bytes=4 * 1024 * 1024),
        )(*after)

    wide = P(None, ("row", "col"))
    line = P(("row", "col"))
    placed = (
        wide,
        wide,
        line,
        line,
        line,
        P("row", "col"),
        P("col", "row"),
        P("row", "col"),
        P(),
        P(),
    )
    return jax.shard_map(
        on_device, mesh=mesh, in_specs=placed, out_specs=(wide, wide), check_vma=False
    )
```
